256 devices in a mesh: tile: 64 (over x, z_hi, y), sec: 4 (over z_lo, core).
Axes of the slice: x: 4, y: 4, z: 8 (z_hi: 4, z_lo: 2; z = z_hi * 2 + z_lo), core: 2. Of those that a mesh axis runs over, the one named last changes fastest.
Arguments:
- pixels: bfloat16 [8, 512, 1024, 256], P('sec', 'tile'), may hold values from -6 to 6
- pred_features: bfloat16 [512, 1024, 128], P('tile'), may hold values from -6 to 6
- offsets: int32 [8, 2, 512, 1024], P('sec', None, 'tile'), may hold values from -1 to 1
- valid_mask: int32 [8, 512, 1024], P('sec', 'tile'), may hold values 0 or 1
- base_shift: float32 [2, 512, 1024], P(None, 'tile'), may hold values from -6 to 6
- w_hidden: bfloat16 [256, 512], replicated, may hold values from -0.375 to 0.375
- w_feature: bfloat16 [512, 128], replicated, may hold values from -0.25 to 0.25
- feat_gain: float32 [128], replicated, may hold values from 0.25 to 1.75
Outputs:
- displacement: float32 [8, 2, 512, 1024], P('sec', None, 'tile')
The draws below stay inside these ranges and needn't reach their ends.
All inputs are finite; a program needn't handle non-finite values. No bound on the sum of `valid_mask` on one device may be relied on, other than what follows from the above.
Results may differ from the reference program's by a relative error of at most 0.0024.
Values may be sent and summed in bfloat16 or wider, within the bound.
A program may use at most 128 MiB of HBM per device.

```python
import jax
import jax.numpy as jnp
from jax import lax

PATCH = 256
HID = 512
FEAT = 128
COLS = 1024
ITERS = 8
SECS = 8
ROWS = 512


def with_ends(array, key, least, top_value):
    longest = array.shape.index(max(array.shape))
    spots = []
    for shift in (0, 1):
        where = [jax.random.randint(jax.random.fold_in(key, axis), (), 0, length) for axis, length in enumerate(array.shape)]
        where[longest] = (where[longest] + shift) % array.shape[longest]
        spots.append(tuple(where))
    return array.at[spots[0]].set(least).at[spots[1]].set(top_value)


def levels(stream_key, shape, cuts, smallest, top_value):
    def one(axis_at, shards_of):
        draws = jax.random.uniform(jax.random.fold_in(jax.random.fold_in(stream_key, 6), axis_at), (shards_of,), jnp.float32, smallest / len(cuts), top_value / len(cuts))
        return jnp.repeat(jnp.exp(draws), shape[axis_at] // shards_of).reshape((-1,) + (1,) * (len(shape) - axis_at - 1))

    level = one(*cuts[0])
    for cut in cuts[1:]:
        level = level * one(*cut)
    return level


def bell_draw(own_key, dims, scale, bound, shards=(), held_as=jnp.bfloat16):
    values = jax.random.normal(own_key, dims, jnp.float32) * scale
    if len(shards) > 0:
        values = levels(own_key, dims, shards, -0.22, 0.18) * values
    return jnp.clip(values, min=-bound, max=bound).astype(held_as)


def setup_inputs(seed: int = 0) -> dict:
    streams_of = jax.random.split(jax.random.key(seed), 9)
    pixels = bell_draw(streams_of[0], (SECS, ROWS, COLS, PATCH), 1.0, 6.0, ((0, 4), (1, 64)))
    pred_features = bell_draw(streams_of[1], (ROWS, COLS, FEAT), 1.0, 6.0, ((0, 64),))
    offsets = with_ends(jax.random.randint(streams_of[2], (SECS, 2, ROWS, COLS), -1, 2), jax.random.fold_in(streams_of[2], 1), -1, 1).astype(jnp.int32)
    valid_mask = with_ends((jax.random.randint(streams_of[3], (SECS, ROWS, COLS), 0, 4) < 3).astype(jnp.int32), jax.random.fold_in(streams_of[3], 1), 0, 1)
    base_shift = bell_draw(streams_of[4], (2, ROWS, COLS), 1.0, 6.0, ((1, 64),), jnp.float32)
    w_hidden = bell_draw(streams_of[5], (PATCH, HID), PATCH ** -0.5, 0.375)
    w_feature = bell_draw(streams_of[6], (HID, FEAT), HID ** -0.5, 0.25)
    feat_gain = jnp.clip(1.0 + 0.15 * jax.random.normal(streams_of[7], (FEAT,), jnp.float32), 0.25, 1.75)
    return dict(pixels=pixels, pred_features=pred_features, offsets=offsets, valid_mask=valid_mask, base_shift=base_shift, w_hidden=w_hidden, w_feature=w_feature, feat_gain=feat_gain)


epsilon = 1e-05
step_size = 0.2
stiffness = 0.5

def encode(section_pixels, w_hidden, w_feature, feat_gain):
    flat = section_pixels.reshape(-1, section_pixels.shape[-1])
    hidden = jax.nn.relu(jnp.dot(flat, w_hidden, preferred_element_type=jnp.float32)).astype(jnp.bfloat16)
    pre = jnp.dot(hidden, w_feature, preferred_element_type=jnp.float32)
    scale = lax.rsqrt(lax.optimization_barrier(jnp.mean(pre * pre, axis=-1, keepdims=True)) + epsilon)
    result = (pre * scale * feat_gain).astype(jnp.bfloat16)
    return result.reshape(section_pixels.shape[:-1] + (w_feature.shape[1],))

def flow_field(feature, ref_rows, offsets):
    rows = feature.shape[-3]
    cols = feature.shape[-2]
    padding = [(0, 0)] * (ref_rows.ndim - 2) + [(2, 2), (0, 0)]
    padded = jnp.pad(ref_rows, padding)
    own = feature.astype(jnp.float32)
    scores = {}
    for shift_y in range(-2, 3):
        for shift_x in range(-2, 3):
            window = padded[..., 2 + shift_y:2 + shift_y + rows, 2 + shift_x:2 + shift_x + cols, :]
            scores[shift_y, shift_x] = lax.optimization_barrier(jnp.sum(own * window.astype(jnp.float32), axis=-1)) / own.shape[-1]
    offset_y = offsets[..., 0, :, :]
    offset_x = offsets[..., 1, :, :]
    total = jnp.ones(offset_y.shape, jnp.float32)
    sum_y = jnp.zeros(offset_y.shape, jnp.float32)
    sum_x = jnp.zeros(offset_y.shape, jnp.float32)
    for near_y in (-1, 0, 1):
        for near_x in (-1, 0, 1):
            picked = jnp.zeros(offset_y.shape, jnp.float32)
            for cand_y in (-1, 0, 1):
                for cand_x in (-1, 0, 1):
                    hit = (offset_y == cand_y) & (offset_x == cand_x)
                    picked = picked + jnp.where(hit, scores[cand_y + near_y, cand_x + near_x], 0.0)
            weight = picked * picked
            total = total + weight
            sum_y = sum_y + weight * near_y
            sum_x = sum_x + weight * near_x
    flow_y = offset_y.astype(jnp.float32) + sum_y / total
    flow_x = offset_x.astype(jnp.float32) + sum_x / total
    return jnp.stack([flow_y, flow_x], axis=-3)

def relax_step(padded, flow, weight):
    center = padded[:, :, 1:-1]
    upper = padded[:, :, :-2]
    lower = padded[:, :, 2:]
    sided = jnp.pad(center, ((0, 0), (0, 0), (0, 0), (1, 1)))
    left_side = sided[..., :-2]
    right_side = sided[..., 2:]
    return center + step_size * (upper + lower + left_side + right_side - 4.0 * center + weight * (flow - center))

def reference(pixels, pred_features, offsets, valid_mask, base_shift, w_hidden, w_feature, feat_gain):
    features = lax.map(lambda section: encode(section, w_hidden, w_feature, feat_gain), pixels)
    references = jnp.concatenate([pred_features[None], features[:-1]], axis=0)
    ref_padded = jnp.pad(references, ((0, 0), (2, 2), (0, 0), (0, 0)))

    def one_flow(items):
        return flow_field(items[0], items[1], items[2])
    flow = lax.map(one_flow, (features, ref_padded, offsets))
    weight = stiffness * valid_mask.astype(jnp.float32)[:, None]
    field = jnp.zeros(flow.shape, jnp.float32)
    for step in range(ITERS):
        padded = jnp.pad(field, ((0, 0), (0, 0), (1, 1), (0, 0)))
        field = relax_step(padded, flow, weight)
    return base_shift[None] + jnp.cumsum(field, axis=0)
```

```python
import jax
import jax.numpy as jnp
from jax import lax
from jax.experimental import pallas as pl
from jax.experimental.pallas import tpu as pltpu
from jax.sharding import PartitionSpec as P

MESH = pl.DeviceIdType.MESH
ITERS = 8
COLS = 1024
PAD = 16
WIDE = COLS + 2 * PAD
HALF = COLS // 2
REACH = 8
ROWS = 8
ALL = ROWS + 2 * REACH
EPS = 1e-05


def remote(src, dst, send, recv, device):
    return pltpu.make_async_remote_copy(
        src_ref=src, dst_ref=dst, send_sem=send, recv_sem=recv, device_id=device, device_id_type=MESH
    )


def body(
    pix_hbm, pred_hbm, offs, mask, w1, w2, gain, out,
    pix, fp, fa, fb, rel, msend, mrecv, flow, fsend, frecv, psend, precv,
    pix_sem, pred_sem, sec_s, sec_r, halo_s, halo_r, rel_s, rel_r, m_s, m_r, f_s, f_r, p_s, p_r,
):
    t = lax.axis_index("tile")
    s = lax.axis_index("sec")
    tiles = lax.axis_size("tile")
    last = tiles - 1
    y = lax.rem(t, 4)
    low = y == 0
    high = y == 3
    has_d = t < last
    has_u = t > 0
    td = jnp.minimum(t + 1, last)
    tu = jnp.maximum(t - 1, 0)
    out_ok = (high & has_d) | (low & has_u)
    rel_dev = jnp.where(high, t - 3, jnp.minimum(t + 3, last))
    in_ok = (high & (rel_dev > 0)) | (low & (rel_dev < last))
    rel_dst = jnp.where(high, jnp.maximum(t - 4, 0), jnp.minimum(t + 4, last))
    fwd = jnp.where(high, jnp.minimum(t + 4, last), jnp.maximum(t - 4, 0))
    next_sec = jnp.minimum(s + 1, 3)

    for q in (1, 0):
        for r in range(ROWS):
            pltpu.make_async_copy(pix_hbm.at[q, r], pix.at[q, r], pix_sem.at[q, r]).start()
    pred_copy = pltpu.make_async_copy(
        pred_hbm, fp.at[pl.ds(2, ROWS), pl.ds(PAD, COLS)], pred_sem
    )

    @pl.when(s == 0)
    def _():
        pred_copy.start()

    zero_side = jnp.zeros((ROWS + 4, PAD, 128), jnp.bfloat16)
    for f in (fp, fa):
        f[:, pl.ds(0, PAD), :] = zero_side
        f[:, pl.ds(PAD + COLS, PAD), :] = zero_side
    zero_rows = jnp.zeros((2, COLS, 128), jnp.bfloat16)

    @pl.when(jnp.logical_not(has_u))
    def _():
        for f in (fp, fa):
            f[pl.ds(0, 2), pl.ds(PAD, COLS), :] = zero_rows
        mrecv[0] = jnp.zeros((16, COLS), jnp.bfloat16)
        for q in range(2):
            frecv[q, 0] = jnp.zeros((16, COLS), jnp.bfloat16)

    @pl.when(jnp.logical_not(has_d))
    def _():
        for f in (fp, fa):
            f[pl.ds(ROWS + 2, 2), pl.ds(PAD, COLS), :] = zero_rows
        mrecv[1] = jnp.zeros((16, COLS), jnp.bfloat16)
        for q in range(2):
            frecv[q, 1] = jnp.zeros((16, COLS), jnp.bfloat16)

    msend[...] = jnp.concatenate([mask[0], mask[1]], axis=0).astype(jnp.float32).astype(jnp.bfloat16)

    barrier = pltpu.get_barrier_semaphore()
    count = jnp.int32(0)
    for ok, device in (
        (has_d, (td, s)),
        (has_u, (tu, s)),
        (out_ok | in_ok, (rel_dev, s)),
        (in_ok, (rel_dst, s)),
        (out_ok, (fwd, s)),
    ):
        count = count + ok.astype(jnp.int32)

        @pl.when(ok)
        def _(device=device):
            pl.semaphore_signal(barrier, inc=1, device_id=device, device_id_type=MESH)

    for k in range(1, 4):
        pl.semaphore_signal(
            barrier, inc=1, device_id=(t, lax.rem(s + k, 4)), device_id_type=MESH
        )
    pl.semaphore_wait(barrier, count + 3)

    def mask_copy(d):
        return remote(msend, mrecv.at[d], m_s.at[d], m_r.at[d], ((td, tu)[d], s))

    def flow_copy(q, d):
        return remote(fsend.at[q], frecv.at[q, d], f_s.at[q, d], f_r.at[q, d], ((td, tu)[d], s))

    def sec_copy(r):
        span = (r + 2, pl.ds(PAD, COLS))
        return remote(fb.at[span], fp.at[span], sec_s.at[r], sec_r.at[r], (t, next_sec))

    feats = (fp, fa)

    def halo_src(u, d, h):
        return feats[u].at[pl.ds(ROWS if d == 0 else 2, 2), pl.ds(PAD + h * HALF, HALF)]

    def halo_dst(u, d, h):
        return feats[u].at[pl.ds(0 if d == 0 else ROWS + 2, 2), pl.ds(PAD + h * HALF, HALF)]

    def direct(u, d, h):
        return remote(
            halo_src(u, d, h), halo_dst(u, d, h), halo_s.at[u, d, h], halo_r.at[u, d, h],
            ((td, tu)[d], s),
        )

    def to_relay(u, d):
        return remote(
            halo_src(u, d, 1), rel.at[u], halo_s.at[u, d, 1], rel_r.at[u], (rel_dev, s)
        )

    def from_relay(u, d):
        return remote(
            rel.at[u], halo_dst(u, d, 1), rel_s.at[u], halo_r.at[u, d, 1], (rel_dst, s)
        )

    ends = (high, low)
    has = (has_d, has_u)

    def start_halo(u):
        for d in range(2):
            edge = ends[d] & has[d]

            @pl.when(edge)
            def _(d=d):
                to_relay(u, d).start()

        for d in range(2):
            edge = ends[d] & has[d]

            @pl.when(has[d])
            def _(d=d):
                direct(u, d, 0).start()

            @pl.when(has[d] & jnp.logical_not(edge))
            def _(d=d):
                direct(u, d, 1).start()

    def relay(u):
        for d in range(2):

            @pl.when(ends[1 - d] & in_ok)
            def _(d=d):
                to_relay(u, d).wait_recv()
                from_relay(u, d).start()

    def wait_halo(u):
        for d in range(2):

            @pl.when(has[1 - d])
            def _(d=d):
                direct(u, d, 0).wait_recv()
                direct(u, d, 1).wait_recv()

    def drain_halo(u):
        for d in range(2):

            @pl.when(has[d])
            def _(d=d):
                direct(u, d, 0).wait_send()
                direct(u, d, 1).wait_send()

            @pl.when(ends[1 - d] & in_ok)
            def _(d=d):
                from_relay(u, d).wait_send()

    for d in range(2):

        @pl.when(has[d])
        def _(d=d):
            mask_copy(d).start()

    @pl.when(s == 0)
    def _():
        pred_copy.wait()
        start_halo(0)

    def encode_row(q, f, r):
        pltpu.make_async_copy(pix_hbm.at[q, r], pix.at[q, r], pix_sem.at[q, r]).wait()

        def block(b, carry):
            x = pix[q, r, pl.ds(pl.multiple_of(b * 256, 256), 256), :]
            hidden = jnp.maximum(
                jnp.dot(x, w1[...], preferred_element_type=jnp.float32), 0.0
            ).astype(jnp.bfloat16)
            pre = jnp.dot(hidden, w2[...], preferred_element_type=jnp.float32)
            scale = lax.rsqrt(jnp.mean(pre * pre, axis=-1, keepdims=True) + EPS)
            f[r + 2, pl.ds(pl.multiple_of(PAD + b * 256, 16), 256), :] = (
                pre * scale * gain[...]
            ).astype(jnp.bfloat16)
            return carry

        lax.fori_loop(0, COLS // 256, block, 0)

    def outer_row(i):
        return jnp.where(i < 2, i, i + 4)

    def encode_last(i, carry):
        r = jnp.where(i < 4, outer_row(i), i - 2)
        encode_row(1, fb, r)

        @pl.when(s < 3)
        def _():
            sec_copy(r).start()

        return carry

    lax.fori_loop(0, ROWS, encode_last, 0)

    @pl.when(s == 0)
    def _():
        relay(0)

    def encode_outer(i, carry):
        encode_row(0, fa, outer_row(i))
        return carry

    def encode_inner(i, carry):
        encode_row(0, fa, i + 2)
        return carry

    lax.fori_loop(0, 4, encode_outer, 0)
    start_halo(1)
    lax.fori_loop(0, 4, encode_inner, 0)

    @pl.when(s > 0)
    def _():
        for r in (0, 1, 6, 7):
            sec_copy(r).wait_recv()
        start_halo(0)

    relay(1)

    sub = lax.broadcasted_iota(jnp.int32, (8, 128), 0)
    lane = lax.broadcasted_iota(jnp.int32, (8, 128), 1)
    turn = lane + (PAD - 2)
    which = (turn + ((sub - turn) & 7)) // 8

    def diagonals(g):
        picked = g[8:16]
        for k in range(2, 19):
            picked = jnp.where(which == k, g[8 * k : 8 * k + 8], picked)
        return picked

    def score_block(q, own, ref, pair, c):
        c0 = pl.multiple_of(c * 128, 128)
        r0 = pair * 2
        rhs = own[pl.ds(r0 + 2, 2), pl.ds(pl.multiple_of(c0 + PAD, 16), 128), :].reshape(256, 128)
        bands = ([], [])
        for k in range(6):
            lhs = ref[r0 + k, pl.ds(c0, 160), :]
            g = lax.dot_general(
                lhs, rhs, (((1,), (1,)), ((), ())), preferred_element_type=jnp.float32
            )
            for j in range(2):
                if 0 <= k - j <= 4:
                    bands[j].append(diagonals(g[:, 128 * j : 128 * j + 128]))
        for j in range(2):
            r = r0 + j
            oy = jnp.broadcast_to(offs[q, 0, pl.ds(r, 1), pl.ds(c0, 128)], (8, 128))
            ox = jnp.broadcast_to(offs[q, 1, pl.ds(r, 1), pl.ds(c0, 128)], (8, 128))
            spin = turn + ox + 1
            band = bands[j]
            for bit in (1, 2, 4):
                take = (spin & bit) != 0
                band = [jnp.where(take, pltpu.roll(v, 8 - bit, 0), v) for v in band]
            weights = []
            for i in range(3):
                near = jnp.where(oy < 0, band[i], jnp.where(oy == 0, band[i + 1], band[i + 2]))
                weights.append(near * near * (2.0**-14))
            every = weights[0] + weights[1] + weights[2]
            tilt = weights[2] - weights[0]
            every1 = pltpu.roll(every, 7, 0)
            every2 = pltpu.roll(every, 6, 0)
            total = 1.0 + (every + every1 + every2)
            sum_y = tilt + pltpu.roll(tilt, 7, 0) + pltpu.roll(tilt, 6, 0)
            sum_x = every2 - every
            flow_y = oy.astype(jnp.float32) + sum_y / total
            flow_x = ox.astype(jnp.float32) + sum_x / total
            flow[q, 0, pl.ds(REACH + r, 1), pl.ds(c0, 128)] = flow_y[0:1]
            flow[q, 1, pl.ds(REACH + r, 1), pl.ds(c0, 128)] = flow_x[0:1]

    def score_pairs(q, own, ref, pairs):
        for pair in pairs:

            def one(c, carry, pair=pair):
                score_block(q, own, ref, pair, c)
                return carry

            lax.fori_loop(0, COLS // 128, one, 0)

    def send_flow(q):
        fsend[q] = jnp.concatenate(
            [flow[q, 0, pl.ds(REACH, ROWS), :], flow[q, 1, pl.ds(REACH, ROWS), :]], axis=0
        ).astype(jnp.bfloat16)
        for d in range(2):

            @pl.when(has[d])
            def _(d=d):
                flow_copy(q, d).start()

    score_pairs(1, fb, fa, (1, 2))

    @pl.when(s > 0)
    def _():
        relay(0)
        for r in (2, 3, 4, 5):
            sec_copy(r).wait_recv()

    score_pairs(0, fa, fp, (1, 2))
    wait_halo(1)
    score_pairs(1, fb, fa, (0, 3))
    send_flow(1)
    wait_halo(0)
    score_pairs(0, fa, fp, (0, 3))
    send_flow(0)

    for d in range(2):

        @pl.when(has[1 - d])
        def _(d=d):
            mask_copy(d).wait_recv()

    row = lax.broadcasted_iota(jnp.int32, (ALL, COLS), 0) + t * ROWS - REACH
    col = lax.broadcasted_iota(jnp.int32, (ALL, COLS), 1)
    inside = jnp.where((row >= 0) & (row < tiles * ROWS), 0.2, 0.0)
    left_ok = jnp.where(col > 0, 1.0, 0.0)
    right_ok = jnp.where(col < COLS - 1, 1.0, 0.0)
    for q in (1, 0):
        for d in range(2):

            @pl.when(has[1 - d])
            def _(q=q, d=d):
                flow_copy(q, d).wait_recv()

        trust = jnp.concatenate(
            [
                mrecv[0, pl.ds(8 * q, 8), :].astype(jnp.float32),
                mask[q].astype(jnp.float32),
                mrecv[1, pl.ds(8 * q, 8), :].astype(jnp.float32),
            ],
            axis=0,
        ) * 0.5
        keep = inside * (1.0 - trust)
        for comp in range(2):
            target = jnp.concatenate(
                [
                    frecv[q, 0, pl.ds(8 * comp, 8), :].astype(jnp.float32),
                    flow[q, comp, pl.ds(REACH, ROWS), :],
                    frecv[q, 1, pl.ds(8 * comp, 8), :].astype(jnp.float32),
                ],
                axis=0,
            )
            drive = inside * trust * target

            def relax(i, field):
                sides = pltpu.roll(field, 1, 1) * left_ok + pltpu.roll(field, COLS - 1, 1) * right_ok
                around = pltpu.roll(field, 1, 0) + pltpu.roll(field, ALL - 1, 0) + sides
                return inside * around + keep * field + drive

            field = lax.fori_loop(1, ITERS, relax, drive)
            flow[q, comp] = field

    mine = pl.ds(REACH, ROWS)
    psend[...] = jnp.concatenate(
        [flow[0, 0, mine, :] + flow[1, 0, mine, :], flow[0, 1, mine, :] + flow[1, 1, mine, :]], axis=0
    ).astype(jnp.bfloat16)

    def prefix_copy(k):
        return remote(
            psend, precv.at[jnp.minimum(s, 2)], p_s.at[k - 1], p_r.at[jnp.minimum(s, 2)],
            (t, jnp.minimum(s + k, 3)),
        )

    for k in (1, 2, 3):

        @pl.when(s + k <= 3)
        def _(k=k):
            prefix_copy(k).start()

    for comp in range(2):
        out[0, comp] = flow[0, comp, mine, :]
        out[1, comp] = flow[0, comp, mine, :] + flow[1, comp, mine, :]

    for source in range(3):

        @pl.when(s > source)
        def _(source=source):
            remote(
                psend, precv.at[source], p_s.at[0], p_r.at[source], (t, next_sec)
            ).wait_recv()
            for comp in range(2):
                add = precv[source, pl.ds(8 * comp, 8), :].astype(jnp.float32)
                for q in range(2):
                    out[q, comp] = out[q, comp] + add

    for d in range(2):

        @pl.when(has[d])
        def _(d=d):
            mask_copy(d).wait_send()
            for q in range(2):
                flow_copy(q, d).wait_send()

    for u in range(2):
        drain_halo(u)

    @pl.when(s < 3)
    def _():
        for r in range(ROWS):
            sec_copy(r).wait_send()

    for k in (1, 2, 3):

        @pl.when(s + k <= 3)
        def _(k=k):
            prefix_copy(k).wait_send()


def shards(pixels, pred_features, offsets, valid_mask, base_shift, w_hidden, w_feature, feat_gain):
    vm = pl.BlockSpec(memory_space=pltpu.VMEM)
    hbm = pl.BlockSpec(memory_space=pl.ANY)
    dma = pltpu.SemaphoreType.DMA
    bf = jnp.bfloat16
    summed = pl.pallas_call(
        body,
        out_shape=jax.ShapeDtypeStruct((2, 2, ROWS, COLS), jnp.float32),
        in_specs=[hbm, hbm, vm, vm, vm, vm, vm],
        out_specs=vm,
        scratch_shapes=[
            pltpu.VMEM((2, ROWS, COLS, 256), bf),
            pltpu.VMEM((ROWS + 4, WIDE, 128), bf),
            pltpu.VMEM((ROWS + 4, WIDE, 128), bf),
            pltpu.VMEM((ROWS + 4, WIDE, 128), bf),
            pltpu.VMEM((2, 2, HALF, 128), bf),
            pltpu.VMEM((16, COLS), bf),
            pltpu.VMEM((2, 16, COLS), bf),
            pltpu.VMEM((2, 2, ALL, COLS), jnp.float32),
            pltpu.VMEM((2, 16, COLS), bf),
            pltpu.VMEM((2, 2, 16, COLS), bf),
            pltpu.VMEM((16, COLS), bf),
            pltpu.VMEM((3, 16, COLS), bf),
            dma((2, ROWS)),
            dma,
            dma((ROWS,)),
            dma((ROWS,)),
            dma((2, 2, 2)),
            dma((2, 2, 2)),
            dma((2,)),
            dma((2,)),
            dma((2,)),
            dma((2,)),
            dma((2, 2)),
            dma((2, 2)),
            dma((3,)),
            dma((3,)),
        ],
        compiler_params=pltpu.CompilerParams(
            collective_id=0, has_side_effects=True, vmem_limit_bytes=48 << 20
        ),
        name="align",
    )(
        pixels, pred_features, offsets, valid_mask, w_hidden, w_feature, feat_gain.reshape(1, 128)
    )
    return summed + base_shift[None]


def solution(mesh):
    in_specs = (
        P("sec", "tile", None, None),
        P("tile", None, None),
        P("sec", None, "tile", None),
        P("sec", "tile", None),
        P(None, "tile", None),
        P(),
        P(),
        P(),
    )
    out_specs = P("sec", None, "tile", None)
    return jax.shard_map(shards, mesh=mesh, in_specs=in_specs, out_specs=out_specs, check_vma=False)
```

```python
import jax
import jax.numpy as jnp
from jax import lax
from jax.experimental import pallas as pl
from jax.experimental.pallas import tpu as pltpu
from jax.sharding import PartitionSpec as P

MESH = pl.DeviceIdType.MESH
ITERS = 8
COLS = 1024
PAD = 16
WIDE = COLS + 2 * PAD
HALF = COLS // 2
SPANS = {
    "full": ((PAD, HALF), (PAD + HALF, HALF)),
    "left": ((PAD, 272), (PAD + 272, 256)),
    "right": ((HALF, 272), (HALF + 272, 256)),
}
REACH = 8
ROWS = 8
ALL = ROWS + 2 * REACH
EPS = 1e-05


def remote(src, dst, send, recv, device):
    return pltpu.make_async_remote_copy(
        src_ref=src, dst_ref=dst, send_sem=send, recv_sem=recv, device_id=device, device_id_type=MESH
    )


def body(
    pix_hbm, pred_hbm, offs_hbm, mask_hbm, w1_hbm, w2_hbm, gain_hbm, out,
    offs, mask, w1, w2, gain, pix, fp, fa, fb, ga, goffs, gflow, bsend, brecv, rel, msend, mrecv, flow, fsend, frecv, psend, precv,
    in_sem, pix_sem, pred_sem, sec_s, sec_r, halo_s, halo_r, rel_s, rel_r, m_s, m_r, f_s, f_r, p_s, p_r, g_s, g_r, x_s, x_r, b_s, b_r,
):
    t = lax.axis_index("tile")
    s = lax.axis_index("sec")
    tiles = lax.axis_size("tile")
    last = tiles - 1
    y = lax.rem(t, 4)
    low = y == 0
    high = y == 3
    has_d = t < last
    has_u = t > 0
    td = jnp.minimum(t + 1, last)
    tu = jnp.maximum(t - 1, 0)
    out_ok = (high & has_d) | (low & has_u)
    rel_dev = jnp.where(high, t - 3, jnp.minimum(t + 3, last))
    in_ok = (high & (rel_dev > 0)) | (low & (rel_dev < last))
    rel_dst = jnp.where(high, jnp.maximum(t - 4, 0), jnp.minimum(t + 4, last))
    fwd = jnp.where(high, jnp.minimum(t + 4, last), jnp.maximum(t - 4, 0))
    next_sec = jnp.minimum(s + 1, 3)

    small = [
        pltpu.make_async_copy(src, dst, in_sem.at[i])
        for i, (src, dst) in enumerate(
            (
                (mask_hbm, mask), (w1_hbm, w1), (w2_hbm, w2), (gain_hbm, gain), (offs_hbm, offs),
            )
        )
    ]
    for copy in small[:4]:
        copy.start()
    outer, inner = (0, 1, 6, 7), (2, 3, 4, 5)
    for q, rows in ((0, outer), (1, outer), (1, inner), (0, inner)):
        for r in rows:
            pltpu.make_async_copy(pix_hbm.at[q, r], pix.at[q, r], pix_sem.at[q, r]).start()
    pred_copy = pltpu.make_async_copy(
        pred_hbm, fp.at[pl.ds(2, ROWS), pl.ds(PAD, COLS)], pred_sem
    )

    small[4].start()

    @pl.when(s == 0)
    def _():
        pred_copy.start()

    zero_side = jnp.zeros((ROWS + 4, PAD, 128), jnp.bfloat16)
    for f in (fp, fa, fb):
        f[:, pl.ds(0, PAD), :] = zero_side
        f[:, pl.ds(PAD + COLS, PAD), :] = zero_side
    zero_rows = jnp.zeros((2, COLS, 128), jnp.bfloat16)

    @pl.when(jnp.logical_not(has_u))
    def _():
        for f in (fp, fa, fb):
            f[pl.ds(0, 2), pl.ds(PAD, COLS), :] = zero_rows
        mrecv[0] = jnp.zeros((16, COLS), jnp.bfloat16)
        brecv[0] = jnp.zeros((8, COLS), jnp.bfloat16)
        for q in range(2):
            frecv[q, 0] = jnp.zeros((16, COLS), jnp.bfloat16)

    @pl.when(jnp.logical_not(has_d))
    def _():
        for f in (fp, fa, fb):
            f[pl.ds(ROWS + 2, 2), pl.ds(PAD, COLS), :] = zero_rows
        mrecv[1] = jnp.zeros((16, COLS), jnp.bfloat16)
        brecv[1] = jnp.zeros((8, COLS), jnp.bfloat16)
        for q in range(2):
            frecv[q, 1] = jnp.zeros((16, COLS), jnp.bfloat16)

    small[0].wait()
    msend[...] = jnp.concatenate([mask[0], mask[1]], axis=0).astype(jnp.float32).astype(jnp.bfloat16)

    barrier = pltpu.get_barrier_semaphore()
    count = jnp.int32(0)
    for ok, device in (
        (has_d, (td, s)),
        (has_u, (tu, s)),
        (out_ok | in_ok, (rel_dev, s)),
        (in_ok, (rel_dst, s)),
        (out_ok, (fwd, s)),
    ):
        count = count + ok.astype(jnp.int32)

        @pl.when(ok)
        def _(device=device):
            pl.semaphore_signal(barrier, inc=1, device_id=device, device_id_type=MESH)

    for k in range(1, 4):
        pl.semaphore_signal(
            barrier, inc=1, device_id=(t, lax.rem(s + k, 4)), device_id_type=MESH
        )
    pl.semaphore_wait(barrier, count + 3)

    def mask_copy(d):
        return remote(msend, mrecv.at[d], m_s.at[d], m_r.at[d], ((td, tu)[d], s))

    def band_copy(d):
        return remote(bsend.at[d], brecv.at[d], b_s.at[d], b_r.at[d], ((td, tu)[d], s))

    def flow_copy(q, d):
        return remote(fsend.at[q], frecv.at[q, d], f_s.at[q, d], f_r.at[q, d], ((td, tu)[d], s))

    def sec_copy(r, h):
        span = (r + 2, pl.ds(PAD, HALF + PAD) if h == 0 else pl.ds(HALF + 2 * PAD, HALF - PAD))
        return remote(fb.at[span], fp.at[span], sec_s.at[r, h], sec_r.at[r, h], (t, next_sec))

    def give_rows(r):
        return remote(
            fa.at[r + 2, pl.ds(PAD + HALF, HALF)], ga.at[r], g_s.at[r], g_r.at[r], (t, 1)
        )

    def give_offs():
        return remote(
            offs.at[0, :, :, pl.ds(HALF, HALF)], goffs, x_s.at[0], x_r.at[0], (t, 1)
        )

    def give_flow():
        return remote(
            gflow, flow.at[0, :, pl.ds(REACH, ROWS), pl.ds(HALF, HALF)], x_s.at[1], x_r.at[1], (t, 2)
        )

    feats = (fp, fa, fb)

    deep = (1, 2, 2)

    def halo_src(u, d, span):
        return feats[u].at[pl.ds(ROWS + 2 - deep[u] if d == 0 else 2, deep[u]), pl.ds(*span)]

    def halo_dst(u, d, span):
        return feats[u].at[pl.ds(2 - deep[u] if d == 0 else ROWS + 2, deep[u]), pl.ds(*span)]

    def direct(u, d, h, kind):
        span = SPANS[kind][h]
        return remote(
            halo_src(u, d, span), halo_dst(u, d, span), halo_s.at[u, d, h], halo_r.at[u, d, h],
            ((td, tu)[d], s),
        )

    def to_relay(u, d, kind):
        span = SPANS[kind][1]
        return remote(
            halo_src(u, d, span), rel.at[u, pl.ds(0, deep[u]), pl.ds(0, span[1])], halo_s.at[u, d, 1], rel_r.at[u],
            (rel_dev, s),
        )

    def from_relay(u, d, kind):
        span = SPANS[kind][1]
        return remote(
            rel.at[u, pl.ds(0, deep[u]), pl.ds(0, span[1])], halo_dst(u, d, span), rel_s.at[u], halo_r.at[u, d, 1],
            (rel_dst, s),
        )

    ends = (high, low)
    has = (has_d, has_u)

    def start_halo(u, kind="full"):
        for d in range(2):
            edge = ends[d] & has[d]

            @pl.when(edge)
            def _(d=d):
                to_relay(u, d, kind).start()

        for d in range(2):
            edge = ends[d] & has[d]

            @pl.when(has[d])
            def _(d=d):
                direct(u, d, 0, kind).start()

            @pl.when(has[d] & jnp.logical_not(edge))
            def _(d=d):
                direct(u, d, 1, kind).start()

    def relay(u, kind="full"):
        for d in range(2):

            @pl.when(ends[1 - d] & in_ok)
            def _(d=d):
                to_relay(u, d, kind).wait_recv()
                from_relay(u, d, kind).start()

    def wait_halo(u, kind="full"):
        for d in range(2):

            @pl.when(has[1 - d])
            def _(d=d):
                direct(u, d, 0, kind).wait_recv()
                direct(u, d, 1, kind).wait_recv()

    def drain_halo(u, kind="full"):
        for d in range(2):

            @pl.when(has[d])
            def _(d=d):
                direct(u, d, 0, kind).wait_send()
                direct(u, d, 1, kind).wait_send()

            @pl.when(ends[1 - d] & in_ok)
            def _(d=d):
                from_relay(u, d, kind).wait_send()

    def first_ref(step):
        pl.when(s != 2)(lambda: step(0))
        pl.when(s == 2)(lambda: step(0, "left"))

    def wait_sec(r):
        sec_copy(r, 0).wait_recv()

        @pl.when(s != 2)
        def _():
            sec_copy(r, 1).wait_recv()

    for d in range(2):

        @pl.when(has[d])
        def _(d=d):
            mask_copy(d).start()

    @pl.when(s == 0)
    def _():
        pred_copy.wait()
        start_halo(0)

    for copy in small[1:]:
        copy.wait()

    def encode_row(q, f, r):
        pltpu.make_async_copy(pix_hbm.at[q, r], pix.at[q, r], pix_sem.at[q, r]).wait()

        hidden = jnp.maximum(
            jnp.dot(pix[q, r], w1[...], preferred_element_type=jnp.float32), 0.0
        ).astype(jnp.bfloat16)
        pre = jnp.dot(hidden, w2[...], preferred_element_type=jnp.float32)
        scale = lax.rsqrt(jnp.mean(pre * pre, axis=-1, keepdims=True) + EPS)
        f[r + 2, pl.ds(PAD, COLS), :] = (pre * scale * gain[...]).astype(jnp.bfloat16)

    def outer_row(i):
        return jnp.where(i < 2, i, i + 4)

    def encode_last(i, carry):
        r = jnp.where(i < 4, outer_row(i), i - 2)
        encode_row(1, fb, r)

        @pl.when(s < 3)
        def _():
            sec_copy(r, 0).start()

        @pl.when((s == 0) | (s == 2))
        def _():
            sec_copy(r, 1).start()

        return carry

    def encode_first(r):
        encode_row(0, fa, r)

        @pl.when(s == 2)
        def _():
            give_rows(r).start()

    def encode_outer(i, carry):
        encode_first(outer_row(i))
        return carry

    def encode_inner(i, carry):
        encode_first(i + 2)
        return carry

    lax.fori_loop(0, 4, encode_outer, 0)
    start_halo(1)

    @pl.when(s == 2)
    def _():
        give_offs().start()

    lax.fori_loop(0, ROWS, encode_last, 0)

    @pl.when(s == 1)
    def _():
        start_halo(2, "right")

    @pl.when(s == 0)
    def _():
        relay(0)

    relay(1)
    lax.fori_loop(0, 4, encode_inner, 0)

    @pl.when(s > 0)
    def _():
        for r in (0, 1, 6, 7):
            wait_sec(r)
        first_ref(start_halo)

    @pl.when(s == 1)
    def _():
        relay(2, "right")

    sub = lax.broadcasted_iota(jnp.int32, (8, 128), 0)
    lane = lax.broadcasted_iota(jnp.int32, (8, 128), 1)
    turn = lane + (PAD - 2)
    which = (turn + ((sub - turn) & 7)) // 8

    def diagonals(g):
        picked = g[8:16]
        for k in range(2, 19):
            picked = jnp.where(which == k, g[8 * k : 8 * k + 8], picked)
        return picked

    def score_block(own, own_r, own_c, ref, offs_at, flow_at, given, pair, c):
        c0 = pl.multiple_of(c * 128, 128)
        r0 = pair * 2
        rhs = own[
            pl.ds(r0 + own_r, 2), pl.ds(pl.multiple_of(c0 + own_c, 16), 128), :
        ].reshape(256, 128)
        bands = ([], [])
        ends_given = {0: 0, 3: 5} if given else {}
        for k in range(6):
            if ends_given.get(pair) == k:
                bands[k // 5].append(brecv[k // 5, :, pl.ds(c0, 128)].astype(jnp.float32))
                continue
            lhs = ref[r0 + k, pl.ds(c0, 160), :]
            g = lax.dot_general(
                lhs, rhs, (((1,), (1,)), ((), ())), preferred_element_type=jnp.float32
            )
            for j in range(2):
                if 0 <= k - j <= 4:
                    bands[j].append(diagonals(g[:, 128 * j : 128 * j + 128]))
        for j in range(2):
            r = r0 + j
            oy = jnp.broadcast_to(offs_at(0, r, c0)[...], (8, 128))
            ox = jnp.broadcast_to(offs_at(1, r, c0)[...], (8, 128))
            spin = turn + ox + 1
            band = bands[j]
            for bit in (1, 2, 4):
                take = (spin & bit) != 0
                band = [jnp.where(take, pltpu.roll(v, 8 - bit, 0), v) for v in band]
            weights = []
            for i in range(3):
                near = jnp.where(oy < 0, band[i], jnp.where(oy == 0, band[i + 1], band[i + 2]))
                weights.append(near * near * (2.0**-14))
            every = weights[0] + weights[1] + weights[2]
            tilt = weights[2] - weights[0]
            every1 = pltpu.roll(every, 7, 0)
            every2 = pltpu.roll(every, 6, 0)
            total = 1.0 + (every + every1 + every2)
            sum_y = tilt + pltpu.roll(tilt, 7, 0) + pltpu.roll(tilt, 6, 0)
            sum_x = every2 - every
            flow_y = oy.astype(jnp.float32) + sum_y / total
            flow_x = ox.astype(jnp.float32) + sum_x / total
            flow_at(0, r, c0)[...] = flow_y[0:1]
            flow_at(1, r, c0)[...] = flow_x[0:1]

    def score_pairs(pairs, blocks, *where):
        for pair in pairs:

            def one(c, carry, pair=pair):
                score_block(*where, pair, c)
                return carry

            lax.fori_loop(*blocks, one, 0, unroll=blocks[1] - blocks[0])

    def offs_of(q):
        return lambda comp, r, c0: offs.at[q, comp, pl.ds(r, 1), pl.ds(c0, 128)]

    def flow_of(q):
        return lambda comp, r, c0: flow.at[q, comp, pl.ds(REACH + r, 1), pl.ds(c0, 128)]

    def score_second(pairs):
        score_pairs(pairs, (0, 8), fb, 2, PAD, fa, offs_of(1), flow_of(1), False)

    def score_first(pairs):
        part = (fa, 2, PAD, fp, offs_of(0), flow_of(0), True)
        score_pairs(pairs, (0, 4), *part)

        @pl.when(s != 2)
        def _():
            score_pairs(pairs, (4, 8), *part)

    def score_given():
        score_pairs(
            (0, 1, 2, 3), (4, 8), ga, 0, -HALF, fb,
            lambda comp, r, c0: goffs.at[comp, pl.ds(r, 1), pl.ds(c0 - HALF, 128)],
            lambda comp, r, c0: gflow.at[comp, pl.ds(r, 1), pl.ds(c0 - HALF, 128)],
            False,
        )

    def score_bands():
        def one(c, carry):
            c0 = pl.multiple_of(c * 128, 128)
            for d in range(2):
                lhs = fp[8 if d == 0 else 3, pl.ds(c0, 160), :]
                rhs = fa[10 if d == 0 else 1, pl.ds(pl.multiple_of(c0 + PAD, 16), 128), :]
                g = lax.dot_general(
                    lhs, rhs, (((1,), (1,)), ((), ())), preferred_element_type=jnp.float32
                )
                bsend[d, :, pl.ds(c0, 128)] = diagonals(g).astype(jnp.bfloat16)
            return carry

        lax.fori_loop(0, 4, one, 0, unroll=4)

        @pl.when(s == 2)
        def _():
            bsend[:, :, pl.ds(HALF, HALF)] = jnp.zeros((2, 8, HALF), jnp.bfloat16)

        @pl.when(s != 2)
        def _():
            lax.fori_loop(4, 8, one, 0, unroll=4)

        for d in range(2):

            @pl.when(has[d])
            def _(d=d):
                band_copy(d).start()

    def send_flow(q):
        fsend[q] = jnp.concatenate(
            [flow[q, 0, pl.ds(REACH, ROWS), :], flow[q, 1, pl.ds(REACH, ROWS), :]], axis=0
        ).astype(jnp.bfloat16)
        for d in range(2):

            @pl.when(has[d])
            def _(d=d):
                flow_copy(q, d).start()

    score_second((1, 2))

    @pl.when(s > 0)
    def _():
        first_ref(relay)

    wait_halo(1)
    score_bands()
    score_second((0, 3))
    send_flow(1)

    @pl.when(s > 0)
    def _():
        for r in (2, 3, 4, 5):
            wait_sec(r)

    score_first((1, 2))

    @pl.when(s == 1)
    def _():
        wait_halo(2, "right")
        give_offs().wait_recv()
        for r in range(ROWS):
            give_rows(r).wait_recv()
        score_given()
        give_flow().start()

    first_ref(wait_halo)
    for d in range(2):

        @pl.when(has[1 - d])
        def _(d=d):
            band_copy(d).wait_recv()

    score_first((0, 3))

    @pl.when(s == 2)
    def _():
        give_flow().wait_recv()

    send_flow(0)

    for d in range(2):

        @pl.when(has[1 - d])
        def _(d=d):
            mask_copy(d).wait_recv()

    row = lax.broadcasted_iota(jnp.int32, (ALL, COLS), 0) + t * ROWS - REACH
    col = lax.broadcasted_iota(jnp.int32, (ALL, COLS), 1)
    inside = jnp.where((row >= 0) & (row < tiles * ROWS), 0.2, 0.0)
    left_ok = jnp.where(col > 0, 1.0, 0.0)
    right_ok = jnp.where(col < COLS - 1, 1.0, 0.0)
    for q in (1, 0):
        for d in range(2):

            @pl.when(has[1 - d])
            def _(q=q, d=d):
                flow_copy(q, d).wait_recv()

        trust = jnp.concatenate(
            [
                mrecv[0, pl.ds(8 * q, 8), :].astype(jnp.float32),
                mask[q].astype(jnp.float32),
                mrecv[1, pl.ds(8 * q, 8), :].astype(jnp.float32),
            ],
            axis=0,
        ) * 0.5
        keep = inside * (1.0 - trust)
        for comp in range(2):
            target = jnp.concatenate(
                [
                    frecv[q, 0, pl.ds(8 * comp, 8), :].astype(jnp.float32),
                    flow[q, comp, pl.ds(REACH, ROWS), :],
                    frecv[q, 1, pl.ds(8 * comp, 8), :].astype(jnp.float32),
                ],
                axis=0,
            )
            drive = inside * trust * target

            def relax(i, field):
                sides = pltpu.roll(field, 1, 1) * left_ok + pltpu.roll(field, COLS - 1, 1) * right_ok
                around = pltpu.roll(field, 1, 0) + pltpu.roll(field, ALL - 1, 0) + sides
                return inside * around + keep * field + drive

            field = lax.fori_loop(1, ITERS, relax, drive)
            flow[q, comp] = field

    mine = pl.ds(REACH, ROWS)
    psend[...] = jnp.concatenate(
        [flow[0, 0, mine, :] + flow[1, 0, mine, :], flow[0, 1, mine, :] + flow[1, 1, mine, :]], axis=0
    ).astype(jnp.bfloat16)

    def prefix_copy(k):
        return remote(
            psend, precv.at[jnp.minimum(s, 2)], p_s.at[k - 1], p_r.at[jnp.minimum(s, 2)],
            (t, jnp.minimum(s + k, 3)),
        )

    for k in (1, 2, 3):

        @pl.when(s + k <= 3)
        def _(k=k):
            prefix_copy(k).start()

    for comp in range(2):
        out[0, comp] = flow[0, comp, mine, :]
        out[1, comp] = flow[0, comp, mine, :] + flow[1, comp, mine, :]

    for source in range(3):

        @pl.when(s > source)
        def _(source=source):
            remote(
                psend, precv.at[source], p_s.at[0], p_r.at[source], (t, next_sec)
            ).wait_recv()
            for comp in range(2):
                add = precv[source, pl.ds(8 * comp, 8), :].astype(jnp.float32)
                for q in range(2):
                    out[q, comp] = out[q, comp] + add

    for d in range(2):

        @pl.when(has[d])
        def _(d=d):
            mask_copy(d).wait_send()
            band_copy(d).wait_send()
            for q in range(2):
                flow_copy(q, d).wait_send()

    drain_halo(1)
    first_ref(drain_halo)

    @pl.when(s == 1)
    def _():
        drain_halo(2, "right")
        give_flow().wait_send()

    @pl.when(s == 2)
    def _():
        give_offs().wait_send()
        for r in range(ROWS):
            give_rows(r).wait_send()

    @pl.when(s < 3)
    def _():
        for r in range(ROWS):
            sec_copy(r, 0).wait_send()

    @pl.when((s == 0) | (s == 2))
    def _():
        for r in range(ROWS):
            sec_copy(r, 1).wait_send()

    for k in (1, 2, 3):

        @pl.when(s + k <= 3)
        def _(k=k):
            prefix_copy(k).wait_send()


def shards(pixels, pred_features, offsets, valid_mask, base_shift, w_hidden, w_feature, feat_gain):
    vm = pl.BlockSpec(memory_space=pltpu.VMEM)
    hbm = pl.BlockSpec(memory_space=pltpu.HBM)
    dma = pltpu.SemaphoreType.DMA
    bf = jnp.bfloat16
    summed = pl.pallas_call(
        body,
        out_shape=jax.ShapeDtypeStruct((2, 2, ROWS, COLS), jnp.float32),
        in_specs=[hbm] * 7,
        out_specs=vm,
        scratch_shapes=[
            pltpu.VMEM((2, 2, ROWS, COLS), jnp.int32),
            pltpu.VMEM((2, ROWS, COLS), jnp.int32),
            pltpu.VMEM((256, 512), bf),
            pltpu.VMEM((512, 128), bf),
            pltpu.VMEM((1, 128), jnp.float32),
            pltpu.VMEM((2, ROWS, COLS, 256), bf),
            pltpu.VMEM((ROWS + 4, WIDE, 128), bf),
            pltpu.VMEM((ROWS + 4, WIDE, 128), bf),
            pltpu.VMEM((ROWS + 4, WIDE, 128), bf),
            pltpu.VMEM((ROWS, HALF, 128), bf),
            pltpu.VMEM((2, ROWS, HALF), jnp.int32),
            pltpu.VMEM((2, ROWS, HALF), jnp.float32),
            pltpu.VMEM((2, 8, COLS), bf),
            pltpu.VMEM((2, 8, COLS), bf),
            pltpu.VMEM((3, 2, HALF, 128), bf),
            pltpu.VMEM((16, COLS), bf),
            pltpu.VMEM((2, 16, COLS), bf),
            pltpu.VMEM((2, 2, ALL, COLS), jnp.float32),
            pltpu.VMEM((2, 16, COLS), bf),
            pltpu.VMEM((2, 2, 16, COLS), bf),
            pltpu.VMEM((16, COLS), bf),
            pltpu.VMEM((3, 16, COLS), bf),
            dma((5,)),
            dma((2, ROWS)),
            dma,
            dma((ROWS, 2)),
            dma((ROWS, 2)),
            dma((3, 2, 2)),
            dma((3, 2, 2)),
            dma((3,)),
            dma((3,)),
            dma((2,)),
            dma((2,)),
            dma((2, 2)),
            dma((2, 2)),
            dma((3,)),
            dma((3,)),
            dma((ROWS,)),
            dma((ROWS,)),
            dma((2,)),
            dma((2,)),
            dma((2,)),
            dma((2,)),
        ],
        compiler_params=pltpu.CompilerParams(
            collective_id=0, has_side_effects=True, vmem_limit_bytes=60 << 20
        ),
        name="align",
    )(
        pixels, pred_features, offsets, valid_mask, w_hidden, w_feature, feat_gain.reshape(1, 128)
    )
    return summed + base_shift[None]


def solution(mesh):
    in_specs = (
        P("sec", "tile", None, None),
        P("tile", None, None),
        P("sec", None, "tile", None),
        P("sec", "tile", None),
        P(None, "tile", None),
        P(),
        P(),
        P(),
    )
    out_specs = P("sec", None, "tile", None)
    return jax.shard_map(shards, mesh=mesh, in_specs=in_specs, out_specs=out_specs, check_vma=False)
```

```python
import jax
import jax.numpy as jnp
from jax import lax
from jax.experimental import pallas as pl
from jax.experimental.pallas import tpu as pltpu
from jax.sharding import PartitionSpec as P

MESH = pl.DeviceIdType.MESH
ITERS = 8
COLS = 1024
PAD = 16
WIDE = COLS + 2 * PAD
HALF = COLS // 2
SPANS = {
    "full": ((PAD, HALF), (PAD + HALF, HALF)),
    "left": ((PAD, 272), (PAD + 272, 256)),
    "right": ((HALF, 272), (HALF + 272, 256)),
}
REACH = 8
ROWS = 8
ALL = ROWS + 2 * REACH
EPS = 1e-05


def remote(src, dst, send, recv, device):
    return pltpu.make_async_remote_copy(
        src_ref=src, dst_ref=dst, send_sem=send, recv_sem=recv, device_id=device, device_id_type=MESH
    )


def body(
    pix_hbm, pred_hbm, offs_hbm, mask_hbm, w1_hbm, w2_hbm, gain_hbm, out,
    offs, mask, w1, w2, gain, pix, fp, fa, fb, ga, goffs, gflow, bsend, brecv, rel, msend, mrecv, flow, fsend, frecv, psend, precv,
    in_sem, pix_sem, pred_sem, sec_s, sec_r, halo_s, halo_r, rel_s, rel_r, m_s, m_r, f_s, f_r, p_s, p_r, g_s, g_r, x_s, x_r, b_s, b_r,
):
    t = lax.axis_index("tile")
    s = lax.axis_index("sec")
    tiles = lax.axis_size("tile")
    last = tiles - 1
    y = lax.rem(t, 4)
    low = y == 0
    high = y == 3
    has_d = t < last
    has_u = t > 0
    td = jnp.minimum(t + 1, last)
    tu = jnp.maximum(t - 1, 0)
    out_ok = (high & has_d) | (low & has_u)
    rel_dev = jnp.where(high, t - 3, jnp.minimum(t + 3, last))
    in_ok = (high & (rel_dev > 0)) | (low & (rel_dev < last))
    rel_dst = jnp.where(high, jnp.maximum(t - 4, 0), jnp.minimum(t + 4, last))
    fwd = jnp.where(high, jnp.minimum(t + 4, last), jnp.maximum(t - 4, 0))
    next_sec = jnp.minimum(s + 1, 3)

    small = [
        pltpu.make_async_copy(src, dst, in_sem.at[i])
        for i, (src, dst) in enumerate(
            (
                (mask_hbm, mask), (w1_hbm, w1), (w2_hbm, w2), (gain_hbm, gain), (offs_hbm, offs),
            )
        )
    ]
    for copy in small[:4]:
        copy.start()
    outer, inner = (0, 1, 6, 7), (2, 3, 4, 5)
    for q, rows in ((0, outer), (1, outer), (1, inner), (0, inner)):
        for r in rows:
            pltpu.make_async_copy(pix_hbm.at[q, r], pix.at[q, r], pix_sem.at[q, r]).start()
    pred_copy = pltpu.make_async_copy(
        pred_hbm, fp.at[pl.ds(2, ROWS), pl.ds(PAD, COLS)], pred_sem
    )

    small[4].start()

    @pl.when(s == 0)
    def _():
        pred_copy.start()

    barrier = pltpu.get_barrier_semaphore()
    count = jnp.int32(0)
    for ok, device in (
        (has_d, (td, s)),
        (has_u, (tu, s)),
        (out_ok | in_ok, (rel_dev, s)),
        (in_ok, (rel_dst, s)),
        (out_ok, (fwd, s)),
    ):
        count = count + ok.astype(jnp.int32)

        @pl.when(ok)
        def _(device=device):
            pl.semaphore_signal(barrier, inc=1, device_id=device, device_id_type=MESH)

    for k in range(1, 4):
        pl.semaphore_signal(
            barrier, inc=1, device_id=(t, lax.rem(s + k, 4)), device_id_type=MESH
        )

    zero_side = jnp.zeros((ROWS + 4, PAD, 128), jnp.bfloat16)
    for f in (fp, fa, fb):
        f[:, pl.ds(0, PAD), :] = zero_side
        f[:, pl.ds(PAD + COLS, PAD), :] = zero_side
    zero_rows = jnp.zeros((2, COLS, 128), jnp.bfloat16)

    @pl.when(jnp.logical_not(has_u))
    def _():
        for f in (fp, fa, fb):
            f[pl.ds(0, 2), pl.ds(PAD, COLS), :] = zero_rows
        mrecv[0] = jnp.zeros((16, COLS), jnp.bfloat16)
        brecv[0] = jnp.zeros((8, COLS), jnp.bfloat16)
        for q in range(2):
            frecv[q, 0] = jnp.zeros((16, COLS), jnp.bfloat16)

    @pl.when(jnp.logical_not(has_d))
    def _():
        for f in (fp, fa, fb):
            f[pl.ds(ROWS + 2, 2), pl.ds(PAD, COLS), :] = zero_rows
        mrecv[1] = jnp.zeros((16, COLS), jnp.bfloat16)
        brecv[1] = jnp.zeros((8, COLS), jnp.bfloat16)
        for q in range(2):
            frecv[q, 1] = jnp.zeros((16, COLS), jnp.bfloat16)

    small[0].wait()
    msend[...] = jnp.concatenate([mask[0], mask[1]], axis=0).astype(jnp.float32).astype(jnp.bfloat16)

    def mask_copy(d):
        return remote(msend, mrecv.at[d], m_s.at[d], m_r.at[d], ((td, tu)[d], s))

    def band_copy(d):
        return remote(bsend.at[d], brecv.at[d], b_s.at[d], b_r.at[d], ((td, tu)[d], s))

    def flow_copy(q, d):
        return remote(fsend.at[q], frecv.at[q, d], f_s.at[q, d], f_r.at[q, d], ((td, tu)[d], s))

    def sec_copy(r, h):
        span = (r + 2, pl.ds(PAD, HALF + PAD) if h == 0 else pl.ds(HALF + 2 * PAD, HALF - PAD))
        return remote(fb.at[span], fp.at[span], sec_s.at[r, h], sec_r.at[r, h], (t, next_sec))

    def give_rows(r):
        return remote(
            fa.at[r + 2, pl.ds(PAD + HALF, HALF)], ga.at[r], g_s.at[r], g_r.at[r], (t, 1)
        )

    def give_offs():
        return remote(
            offs.at[0, :, :, pl.ds(HALF, HALF)], goffs, x_s.at[0], x_r.at[0], (t, 1)
        )

    def give_flow():
        return remote(
            gflow, flow.at[0, :, pl.ds(REACH, ROWS), pl.ds(HALF, HALF)], x_s.at[1], x_r.at[1], (t, 2)
        )

    feats = (fp, fa, fb)

    deep = (1, 2, 2)

    def halo_src(u, d, span, row=None):
        start = ROWS + 2 - deep[u] if d == 0 else 2
        rows = pl.ds(start, deep[u]) if row is None else pl.ds(start + row, 1)
        return feats[u].at[rows, pl.ds(*span)]

    def halo_dst(u, d, span, row=None):
        start = 2 - deep[u] if d == 0 else ROWS + 2
        rows = pl.ds(start, deep[u]) if row is None else pl.ds(start + row, 1)
        return feats[u].at[rows, pl.ds(*span)]

    def direct(u, d, h, kind):
        span = SPANS[kind][h]
        return remote(
            halo_src(u, d, span), halo_dst(u, d, span), halo_s.at[u, d, h], halo_r.at[u, d, h],
            ((td, tu)[d], s),
        )

    def to_relay(u, d, kind, row):
        span = SPANS[kind][1]
        return remote(
            halo_src(u, d, span, row), rel.at[u, pl.ds(row, 1), pl.ds(0, span[1])],
            halo_s.at[u, d, 1], rel_r.at[u, row], (rel_dev, s),
        )

    def from_relay(u, d, kind, row):
        span = SPANS[kind][1]
        return remote(
            rel.at[u, pl.ds(row, 1), pl.ds(0, span[1])], halo_dst(u, d, span, row),
            rel_s.at[u, row], halo_r.at[u, d, 1], (rel_dst, s),
        )

    ends = (high, low)
    has = (has_d, has_u)

    def start_halo(u, kind="full"):
        for d in range(2):
            edge = ends[d] & has[d]

            @pl.when(edge)
            def _(d=d):
                for row in range(deep[u]):
                    to_relay(u, d, kind, row).start()

        for d in range(2):
            edge = ends[d] & has[d]

            @pl.when(has[d])
            def _(d=d):
                direct(u, d, 0, kind).start()

            @pl.when(has[d] & jnp.logical_not(edge))
            def _(d=d):
                direct(u, d, 1, kind).start()

    def relay(u, kind="full", rows=None):
        for d in range(2):

            @pl.when(ends[1 - d] & in_ok)
            def _(d=d):
                for row in rows or range(deep[u]):
                    to_relay(u, d, kind, row).wait_recv()
                    from_relay(u, d, kind, row).start()

    def wait_halo(u, kind="full"):
        for d in range(2):

            @pl.when(has[1 - d])
            def _(d=d):
                direct(u, d, 0, kind).wait_recv()
                direct(u, d, 1, kind).wait_recv()

    def drain_halo(u, kind="full"):
        for d in range(2):

            @pl.when(has[d])
            def _(d=d):
                direct(u, d, 0, kind).wait_send()
                direct(u, d, 1, kind).wait_send()

            @pl.when(ends[1 - d] & in_ok)
            def _(d=d):
                for row in range(deep[u]):
                    from_relay(u, d, kind, row).wait_send()

    def first_ref(step):
        pl.when(s != 2)(lambda: step(0))
        pl.when(s == 2)(lambda: step(0, "left"))

    def wait_sec(r):
        sec_copy(r, 0).wait_recv()

        @pl.when(s != 2)
        def _():
            sec_copy(r, 1).wait_recv()

    pl.semaphore_wait(barrier, count + 3)

    @pl.when(s == 0)
    def _():
        pred_copy.wait()
        start_halo(0)

    for d in range(2):

        @pl.when(has[d])
        def _(d=d):
            mask_copy(d).start()

    for copy in small[1:]:
        copy.wait()

    def encode_row(q, f, r):
        pltpu.make_async_copy(pix_hbm.at[q, r], pix.at[q, r], pix_sem.at[q, r]).wait()
        hidden = jnp.maximum(
            jnp.dot(pix[q, r], w1[...], preferred_element_type=jnp.float32), 0.0
        ).astype(jnp.bfloat16)
        pre = jnp.dot(hidden, w2[...], preferred_element_type=jnp.float32)
        scale = lax.rsqrt(jnp.mean(pre * pre, axis=-1, keepdims=True) + EPS)
        f[r + 2, pl.ds(PAD, COLS), :] = (pre * scale * gain[...]).astype(jnp.bfloat16)

    def outer_row(i):
        return jnp.where(i < 2, i, i + 4)

    def encode_outer(i, carry):
        encode_row(0, fa, outer_row(i))
        return carry

    lax.fori_loop(0, 4, encode_outer, 0)
    def send_last(r):
        @pl.when(s < 3)
        def _():
            sec_copy(r, 0).start()

        @pl.when((s == 0) | (s == 2))
        def _():
            sec_copy(r, 1).start()

    start_halo(1)

    @pl.when(s == 2)
    def _():
        give_offs().start()
        for r in (0, 1, 6, 7):
            give_rows(r).start()

    def encode_last_outer(i, carry):
        encode_row(1, fb, outer_row(i))
        send_last(outer_row(i))
        return carry

    def encode_last_inner(i, carry):
        encode_row(1, fb, i + 2)
        send_last(i + 2)
        return carry

    def encode_inner(i, carry):
        encode_row(0, fa, i + 2)

        @pl.when(s == 2)
        def _():
            give_rows(i + 2).start()

        return carry

    lax.fori_loop(0, 4, encode_last_outer, 0)

    @pl.when(s == 1)
    def _():
        start_halo(2, "right")

    @pl.when(s == 0)
    def _():
        relay(0)

    lax.fori_loop(0, 2, encode_last_inner, 0)
    relay(1, rows=(0,))
    lax.fori_loop(2, 4, encode_last_inner, 0)
    relay(1, rows=(1,))

    @pl.when((s == 1) | (s == 3))
    def _():
        for r in (0, 1, 6, 7):
            wait_sec(r)
        start_halo(0)

    lax.fori_loop(0, 4, encode_inner, 0)

    @pl.when(s == 2)
    def _():
        for r in (0, 1, 6, 7):
            wait_sec(r)
        start_halo(0, "left")

    @pl.when(s == 1)
    def _():
        relay(2, "right")

    sub = lax.broadcasted_iota(jnp.int32, (8, 128), 0)
    lane = lax.broadcasted_iota(jnp.int32, (8, 128), 1)
    turn = lane + (PAD - 2)
    which = (turn + ((sub - turn) & 7)) // 8

    def diagonals(g):
        picked = g[8:16]
        for k in range(2, 19):
            picked = jnp.where(which == k, g[8 * k : 8 * k + 8], picked)
        return picked

    def score_block(own, own_r, own_c, ref, offs_at, flow_at, given, pair, c):
        c0 = pl.multiple_of(c * 128, 128)
        r0 = pair * 2
        rhs = own[
            pl.ds(r0 + own_r, 2), pl.ds(pl.multiple_of(c0 + own_c, 16), 128), :
        ].reshape(256, 128)
        bands = ([], [])
        ends_given = {0: 0, 3: 5} if given else {}
        for k in range(6):
            if ends_given.get(pair) == k:
                bands[k // 5].append(brecv[k // 5, :, pl.ds(c0, 128)].astype(jnp.float32))
                continue
            lhs = ref[r0 + k, pl.ds(c0, 160), :]
            g = lax.dot_general(
                lhs, rhs, (((1,), (1,)), ((), ())), preferred_element_type=jnp.float32
            )
            for j in range(2):
                if 0 <= k - j <= 4:
                    bands[j].append(diagonals(g[:, 128 * j : 128 * j + 128]))
        for j in range(2):
            r = r0 + j
            oy = jnp.broadcast_to(offs_at(0, r, c0)[...], (8, 128))
            ox = jnp.broadcast_to(offs_at(1, r, c0)[...], (8, 128))
            spin = turn + ox + 1
            band = bands[j]
            for bit in (1, 2, 4):
                take = (spin & bit) != 0
                band = [jnp.where(take, pltpu.roll(v, 8 - bit, 0), v) for v in band]
            weights = []
            for i in range(3):
                near = jnp.where(oy < 0, band[i], jnp.where(oy == 0, band[i + 1], band[i + 2]))
                weights.append(near * near * (2.0**-14))
            every = weights[0] + weights[1] + weights[2]
            tilt = weights[2] - weights[0]
            every1 = pltpu.roll(every, 7, 0)
            every2 = pltpu.roll(every, 6, 0)
            total = 1.0 + (every + every1 + every2)
            sum_y = tilt + pltpu.roll(tilt, 7, 0) + pltpu.roll(tilt, 6, 0)
            sum_x = every2 - every
            flow_y = oy.astype(jnp.float32) + sum_y / total
            flow_x = ox.astype(jnp.float32) + sum_x / total
            flow_at(0, r, c0)[...] = flow_y[0:1]
            flow_at(1, r, c0)[...] = flow_x[0:1]

    def score_pairs(pairs, blocks, *where):
        for pair in pairs:

            def one(c, carry, pair=pair):
                score_block(*where, pair, c)
                return carry

            lax.fori_loop(*blocks, one, 0, unroll=blocks[1] - blocks[0])

    def offs_of(q):
        return lambda comp, r, c0: offs.at[q, comp, pl.ds(r, 1), pl.ds(c0, 128)]

    def flow_of(q):
        return lambda comp, r, c0: flow.at[q, comp, pl.ds(REACH + r, 1), pl.ds(c0, 128)]

    def score_second(pairs):
        score_pairs(pairs, (0, 8), fb, 2, PAD, fa, offs_of(1), flow_of(1), False)

    def score_first(pairs):
        part = (fa, 2, PAD, fp, offs_of(0), flow_of(0), True)
        score_pairs(pairs, (0, 4), *part)

        @pl.when(s != 2)
        def _():
            score_pairs(pairs, (4, 8), *part)

    def score_given():
        score_pairs(
            (0, 1, 2, 3), (4, 8), ga, 0, -HALF, fb,
            lambda comp, r, c0: goffs.at[comp, pl.ds(r, 1), pl.ds(c0 - HALF, 128)],
            lambda comp, r, c0: gflow.at[comp, pl.ds(r, 1), pl.ds(c0 - HALF, 128)],
            False,
        )

    def score_bands():
        def one(c, carry):
            c0 = pl.multiple_of(c * 128, 128)
            for d in range(2):
                lhs = fp[8 if d == 0 else 3, pl.ds(c0, 160), :]
                rhs = fa[10 if d == 0 else 1, pl.ds(pl.multiple_of(c0 + PAD, 16), 128), :]
                g = lax.dot_general(
                    lhs, rhs, (((1,), (1,)), ((), ())), preferred_element_type=jnp.float32
                )
                bsend[d, :, pl.ds(c0, 128)] = diagonals(g).astype(jnp.bfloat16)
            return carry

        lax.fori_loop(0, 4, one, 0, unroll=4)

        @pl.when(s == 2)
        def _():
            bsend[:, :, pl.ds(HALF, HALF)] = jnp.zeros((2, 8, HALF), jnp.bfloat16)

        @pl.when(s != 2)
        def _():
            lax.fori_loop(4, 8, one, 0, unroll=4)

        for d in range(2):

            @pl.when(has[d])
            def _(d=d):
                band_copy(d).start()

    def send_flow(q):
        fsend[q] = jnp.concatenate(
            [flow[q, 0, pl.ds(REACH, ROWS), :], flow[q, 1, pl.ds(REACH, ROWS), :]], axis=0
        ).astype(jnp.bfloat16)
        for d in range(2):

            @pl.when(has[d])
            def _(d=d):
                flow_copy(q, d).start()

    score_second((1, 2))

    @pl.when(s > 0)
    def _():
        first_ref(relay)

    wait_halo(1)
    score_bands()
    score_second((0, 3))
    send_flow(1)

    @pl.when(s > 0)
    def _():
        for r in (2, 3, 4, 5):
            wait_sec(r)

    score_first((1, 2))

    @pl.when(s == 1)
    def _():
        wait_halo(2, "right")
        give_offs().wait_recv()
        for r in range(ROWS):
            give_rows(r).wait_recv()
        score_given()
        give_flow().start()

    first_ref(wait_halo)
    for d in range(2):

        @pl.when(has[1 - d])
        def _(d=d):
            band_copy(d).wait_recv()

    score_first((0, 3))

    @pl.when(s == 2)
    def _():
        give_flow().wait_recv()

    send_flow(0)

    for d in range(2):

        @pl.when(has[1 - d])
        def _(d=d):
            mask_copy(d).wait_recv()

    row = lax.broadcasted_iota(jnp.int32, (ALL, COLS), 0) + t * ROWS - REACH
    col = lax.broadcasted_iota(jnp.int32, (ALL, COLS), 1)
    inside = jnp.where((row >= 0) & (row < tiles * ROWS), 0.2, 0.0)
    left_ok = jnp.where(col > 0, 1.0, 0.0)
    right_ok = jnp.where(col < COLS - 1, 1.0, 0.0)
    for q in (1, 0):
        for d in range(2):

            @pl.when(has[1 - d])
            def _(q=q, d=d):
                flow_copy(q, d).wait_recv()

        trust = jnp.concatenate(
            [
                mrecv[0, pl.ds(8 * q, 8), :].astype(jnp.float32),
                mask[q].astype(jnp.float32),
                mrecv[1, pl.ds(8 * q, 8), :].astype(jnp.float32),
            ],
            axis=0,
        ) * 0.5
        keep = inside * (1.0 - trust)
        for comp in range(2):
            target = jnp.concatenate(
                [
                    frecv[q, 0, pl.ds(8 * comp, 8), :].astype(jnp.float32),
                    flow[q, comp, pl.ds(REACH, ROWS), :],
                    frecv[q, 1, pl.ds(8 * comp, 8), :].astype(jnp.float32),
                ],
                axis=0,
            )
            drive = inside * trust * target

            def relax(i, field):
                sides = pltpu.roll(field, 1, 1) * left_ok + pltpu.roll(field, COLS - 1, 1) * right_ok
                around = pltpu.roll(field, 1, 0) + pltpu.roll(field, ALL - 1, 0) + sides
                return inside * around + keep * field + drive

            field = lax.fori_loop(1, ITERS, relax, drive)
            flow[q, comp] = field

    mine = pl.ds(REACH, ROWS)
    psend[...] = jnp.concatenate(
        [flow[0, 0, mine, :] + flow[1, 0, mine, :], flow[0, 1, mine, :] + flow[1, 1, mine, :]], axis=0
    ).astype(jnp.bfloat16)

    def prefix_copy(k):
        return remote(
            psend, precv.at[jnp.minimum(s, 2)], p_s.at[k - 1], p_r.at[jnp.minimum(s, 2)],
            (t, jnp.minimum(s + k, 3)),
        )

    for k in (1, 2, 3):

        @pl.when(s + k <= 3)
        def _(k=k):
            prefix_copy(k).start()

    for comp in range(2):
        out[0, comp] = flow[0, comp, mine, :]
        out[1, comp] = flow[0, comp, mine, :] + flow[1, comp, mine, :]

    for source in range(3):

        @pl.when(s > source)
        def _(source=source):
            remote(
                psend, precv.at[source], p_s.at[0], p_r.at[source], (t, next_sec)
            ).wait_recv()
            for comp in range(2):
                add = precv[source, pl.ds(8 * comp, 8), :].astype(jnp.float32)
                for q in range(2):
                    out[q, comp] = out[q, comp] + add

    for d in range(2):

        @pl.when(has[d])
        def _(d=d):
            mask_copy(d).wait_send()
            band_copy(d).wait_send()
            for q in range(2):
                flow_copy(q, d).wait_send()

    drain_halo(1)
    first_ref(drain_halo)

    @pl.when(s == 1)
    def _():
        drain_halo(2, "right")
        give_flow().wait_send()

    @pl.when(s == 2)
    def _():
        give_offs().wait_send()
        for r in range(ROWS):
            give_rows(r).wait_send()

    @pl.when(s < 3)
    def _():
        for r in range(ROWS):
            sec_copy(r, 0).wait_send()

    @pl.when((s == 0) | (s == 2))
    def _():
        for r in range(ROWS):
            sec_copy(r, 1).wait_send()

    for k in (1, 2, 3):

        @pl.when(s + k <= 3)
        def _(k=k):
            prefix_copy(k).wait_send()


def shards(pixels, pred_features, offsets, valid_mask, base_shift, w_hidden, w_feature, feat_gain):
    vm = pl.BlockSpec(memory_space=pltpu.VMEM)
    hbm = pl.BlockSpec(memory_space=pltpu.HBM)
    dma = pltpu.SemaphoreType.DMA
    bf = jnp.bfloat16
    summed = pl.pallas_call(
        body,
        out_shape=jax.ShapeDtypeStruct((2, 2, ROWS, COLS), jnp.float32),
        in_specs=[hbm] * 7,
        out_specs=vm,
        scratch_shapes=[
            pltpu.VMEM((2, 2, ROWS, COLS), jnp.int32),
            pltpu.VMEM((2, ROWS, COLS), jnp.int32),
            pltpu.VMEM((256, 512), bf),
            pltpu.VMEM((512, 128), bf),
            pltpu.VMEM((1, 128), jnp.float32),
            pltpu.VMEM((2, ROWS, COLS, 256), bf),
            pltpu.VMEM((ROWS + 4, WIDE, 128), bf),
            pltpu.VMEM((ROWS + 4, WIDE, 128), bf),
            pltpu.VMEM((ROWS + 4, WIDE, 128), bf),
            pltpu.VMEM((ROWS, HALF, 128), bf),
            pltpu.VMEM((2, ROWS, HALF), jnp.int32),
            pltpu.VMEM((2, ROWS, HALF), jnp.float32),
            pltpu.VMEM((2, 8, COLS), bf),
            pltpu.VMEM((2, 8, COLS), bf),
            pltpu.VMEM((3, 2, HALF, 128), bf),
            pltpu.VMEM((16, COLS), bf),
            pltpu.VMEM((2, 16, COLS), bf),
            pltpu.VMEM((2, 2, ALL, COLS), jnp.float32),
            pltpu.VMEM((2, 16, COLS), bf),
            pltpu.VMEM((2, 2, 16, COLS), bf),
            pltpu.VMEM((16, COLS), bf),
            pltpu.VMEM((3, 16, COLS), bf),
            dma((5,)),
            dma((2, ROWS)),
            dma,
            dma((ROWS, 2)),
            dma((ROWS, 2)),
            dma((3, 2, 2)),
            dma((3, 2, 2)),
            dma((3, 2)),
            dma((3, 2)),
            dma((2,)),
            dma((2,)),
            dma((2, 2)),
            dma((2, 2)),
            dma((3,)),
            dma((3,)),
            dma((ROWS,)),
            dma((ROWS,)),
            dma((2,)),
            dma((2,)),
            dma((2,)),
            dma((2,)),
        ],
        compiler_params=pltpu.CompilerParams(
            collective_id=0, has_side_effects=True, vmem_limit_bytes=60 << 20
        ),
        name="align",
    )(
        pixels, pred_features, offsets, valid_mask, w_hidden, w_feature, feat_gain.reshape(1, 128)
    )
    return summed + base_shift[None]


def solution(mesh):
    in_specs = (
        P("sec", "tile", None, None),
        P("tile", None, None),
        P("sec", None, "tile", None),
        P("sec", "tile", None),
        P(None, "tile", None),
        P(),
        P(),
        P(),
    )
    out_specs = P("sec", None, "tile", None)
    return jax.shard_map(shards, mesh=mesh, in_specs=in_specs, out_specs=out_specs, check_vma=False)
```
